32 devices in a mesh: dap: 8 (over y, x, core), dp: 4 (over z).
Axes of the slice: x: 2, y: 2, z: 4, core: 2. Of those that a mesh axis runs over, the one named last changes fastest.
Arguments:
- pair: bfloat16 [64, 16, 128], P(('dp', 'dap')), parts along dimension 0, may hold values from -6 to 6
- pair_mask: int32 [64, 16], P(('dp', 'dap')), parts along dimension 0, may hold values from 0 to 1, as said below
- w_left: bfloat16 [128, 256], replicated, may hold values from -0.5 to 0.5
- w_right: bfloat16 [128, 256], replicated, may hold values from -0.5 to 0.5
- w_tri_gate: bfloat16 [128, 128], replicated, may hold values from -0.5 to 0.5
- w_tri_out: bfloat16 [128, 128], replicated, may hold values from -0.5 to 0.5
- w_attend: bfloat16 [128, 512], replicated, may hold values from -0.5 to 0.5
- w_bias: bfloat16 [128, 4], replicated
- w_att_out: bfloat16 [128, 128], replicated, may hold values from -0.5 to 0.5
Outputs:
- pair_out: float32 [64, 16, 128], P('dp', 'dap'), parts along dimension 0
The draws below stay inside these ranges and needn't reach their ends.
There are 4 independent parts, one for each index of `dp`. The reference program is written for one: setup_inputs(seed, part) draws one part's arguments, and reference() takes and returns one part's arrays. A program takes and returns all parts, laid end to end along the dimension named above; an argument that names none is the same for every part. Nothing has to cross between parts.
Inputs may be any that keep to these rules, and one draw needn't show every extreme that they name: pair_mask[i, i] = 1 for every residue i.
All inputs are finite; a program needn't handle non-finite values.
Results may differ from the reference program's by a relative error of at most 0.014.
The reference program's roundings to bfloat16 on the way (of `zn`, `left_edge`, `right_edge`, `tn`, `yn`, `bias`, `weights` and `att`) count: a program that leaves them out, or rounds other values in their place, can miss the bound.
Values may be sent and summed in bfloat16 or wider, within the bound.
No kernel may reach another device: no remote copies, remote signals or barrier semaphores. Data moves between devices by JAX's collectives and lax.ppermute only.
A program may use at most 128 MiB of HBM per device.

```python
import jax
import jax.numpy as jnp
from jax import lax

C = 128
H = 128
HEADS = 4
HEAD_DIM = 32
N = 16


def draw_pair_mask(key, part):
    levels = jax.random.randint(key, (N, N), 0, 8)
    index = jnp.arange(N)
    diagonal = index[:, None] == index[None, :]
    return jnp.where(diagonal, 1, (levels > 0).astype(jnp.int32)).astype(jnp.int32)


def draw_w_bias(key, part):
    base = jax.random.normal(key, (C, HEADS), jnp.float32) / jnp.sqrt(jnp.float32(C))
    return base.astype(jnp.bfloat16)


def shard_levels(key, shape, pieces, smallest, high):
    def one(axis_at, shards_of):
        draws = jax.random.uniform(jax.random.fold_in(jax.random.fold_in(key, 6), axis_at), (shards_of,), jnp.float32, smallest / len(pieces), high / len(pieces))
        return jnp.repeat(jnp.exp(draws), shape[axis_at] // shards_of).reshape((-1,) + (1,) * (len(shape) - axis_at - 1))

    level = one(*pieces[0])
    for cut in pieces[1:]:
        level = level * one(*cut)
    return level


def scatter_about(rng, dims, scale, limit, shards=(), kind=jnp.bfloat16):
    array = jax.random.normal(rng, dims, jnp.float32) * scale
    if len(shards) > 0:
        array = shard_levels(rng, dims, shards, -0.22, 0.18) * array
    return jnp.clip(array, min=-limit, max=limit).astype(kind)


def setup_inputs(seed: int = 0, part: int = 0) -> dict:
    streams_of = jax.random.split(jax.random.key(seed), 10)
    part_splits = jax.random.split(jax.random.fold_in(streams_of[9], part), 10)
    return {
        "pair": scatter_about(part_splits[0], (N, N, C), 1.0, 6.0, ((0, 8),)),
        "pair_mask": draw_pair_mask(jax.random.fold_in(jax.random.fold_in(streams_of[9], part), 71), part),
        "w_left": scatter_about(streams_of[2], (C, 2 * H), C ** -0.5, 0.5),
        "w_right": scatter_about(streams_of[3], (C, 2 * H), C ** -0.5, 0.5),
        "w_tri_gate": scatter_about(streams_of[4], (C, C), C ** -0.5, 0.5),
        "w_tri_out": scatter_about(streams_of[5], (H, C), H ** -0.5, 0.5),
        "w_attend": scatter_about(streams_of[6], (C, 4 * HEADS * HEAD_DIM), C ** -0.5, 0.5),
        "w_bias": draw_w_bias(jax.random.fold_in(streams_of[9], 71), part),
        "w_att_out": scatter_about(streams_of[8], (HEADS * HEAD_DIM, C), (HEADS * HEAD_DIM) ** -0.5, 0.5),
    }


def layer_norm(x):
    x = x.astype(jnp.float32)
    mean = lax.optimization_barrier(jnp.mean(x, axis=-1, keepdims=True))
    var = lax.optimization_barrier(jnp.mean((x - mean) * (x - mean), axis=-1, keepdims=True))
    return (x - mean) / jnp.sqrt(var + 1e-05)

def matmul(x, w):
    flat = x.reshape(-1, x.shape[-1])
    return jnp.dot(flat, w, preferred_element_type=jnp.float32).reshape(x.shape[:-1] + (w.shape[1],))

def reference(pair, pair_mask, w_left, w_right, w_tri_gate, w_tri_out, w_attend, w_bias, w_att_out):
    hidden = w_tri_out.shape[0]
    inner = w_att_out.shape[0]
    heads = w_bias.shape[1]
    head_dim = inner // heads
    rows = pair.shape[0]
    maskf = pair_mask.astype(jnp.float32)
    zn = layer_norm(pair).astype(jnp.bfloat16)
    left = matmul(zn, w_left)
    left_edge = (jax.nn.sigmoid(left[..., :hidden]) * left[..., hidden:] * maskf[..., None]).astype(jnp.bfloat16)
    right = matmul(zn, w_right)
    right_edge = (jax.nn.sigmoid(right[..., :hidden]) * right[..., hidden:] * maskf[..., None]).astype(jnp.bfloat16)
    tri = jnp.einsum('ikc,jkc->ijc', left_edge.astype(jnp.float32), right_edge.astype(jnp.float32))
    tn = layer_norm(tri).astype(jnp.bfloat16)
    update = jax.nn.sigmoid(matmul(zn, w_tri_gate)) * matmul(tn, w_tri_out)
    pair1 = pair.astype(jnp.float32) + update
    yn = layer_norm(pair1).astype(jnp.bfloat16)
    proj = matmul(yn, w_attend)
    query = proj[..., :inner].astype(jnp.bfloat16).reshape(rows, rows, heads, head_dim)
    keys = proj[..., inner:2 * inner].astype(jnp.bfloat16).reshape(rows, rows, heads, head_dim)
    values = proj[..., 2 * inner:3 * inner].astype(jnp.bfloat16).reshape(rows, rows, heads, head_dim)
    gate = jax.nn.sigmoid(proj[..., 3 * inner:])
    bias = jnp.einsum('kic,ch->hki', yn.astype(jnp.float32), w_bias.astype(jnp.float32)).astype(jnp.bfloat16)
    scores = jnp.einsum('ijhd,kjhd->jhki', query.astype(jnp.float32), keys.astype(jnp.float32)) / jnp.sqrt(jnp.float32(head_dim))
    scores = scores + bias.astype(jnp.float32)[None]
    live = jnp.transpose(maskf)[:, None, :, None]
    scores = jnp.where(live > 0.5, scores, jnp.float32(-1000000000.0))
    weights = jax.nn.softmax(scores, axis=2).astype(jnp.bfloat16)
    summed = jnp.einsum('jhki,kjhd->ijhd', weights.astype(jnp.float32), values.astype(jnp.float32)).reshape(rows, rows, inner)
    att = (gate * summed).astype(jnp.bfloat16)
    return pair1 + matmul(att, w_att_out)
```

```python
import functools

import jax
import jax.numpy as jnp
from jax import lax
from jax.experimental import pallas as pl
from jax.experimental.pallas import tpu as pltpu
from jax.sharding import PartitionSpec as P

F32 = jnp.float32
BF16 = jnp.bfloat16
VMEM = pl.BlockSpec(memory_space=pltpu.VMEM)
MODE = "a2a"
LIMIT = 8 * 1024 * 1024


def layer_norm(x):
    x = x.astype(jnp.float32)
    mean = jnp.mean(x, axis=-1, keepdims=True)
    var = jnp.mean((x - mean) * (x - mean), axis=-1, keepdims=True)
    return (x - mean) / jnp.sqrt(var + 1e-05)


def matmul(x, w):
    flat = x.reshape(-1, x.shape[-1])
    return jnp.dot(flat, w, preferred_element_type=jnp.float32).reshape(
        x.shape[:-1] + (w.shape[1],)
    )


def edges(zn, weight, maskf, hidden):
    both = matmul(zn, weight)
    return (jax.nn.sigmoid(both[..., :hidden]) * both[..., hidden:] * maskf[..., None]).astype(
        jnp.bfloat16
    )


def triangle_update(pair_part, zn_part, tri, w_tri_gate, w_tri_out):
    tn = layer_norm(tri).astype(jnp.bfloat16)
    update = jax.nn.sigmoid(matmul(zn_part, w_tri_gate)) * matmul(tn, w_tri_out)
    return pair_part.astype(jnp.float32) + update


def attention(pair1, mask_cols, w_attend, w_bias, w_att_out):
    inner = w_att_out.shape[0]
    heads = w_bias.shape[1]
    head_dim = inner // heads
    total, local = (pair1.shape[0], pair1.shape[1])
    yn = layer_norm(pair1).astype(jnp.bfloat16)
    proj = matmul(yn, w_attend)
    query = proj[..., :inner].astype(jnp.bfloat16).reshape(total, local, heads, head_dim)
    keys = proj[..., inner : 2 * inner].astype(jnp.bfloat16).reshape(total, local, heads, head_dim)
    values = (
        proj[..., 2 * inner : 3 * inner].astype(jnp.bfloat16).reshape(total, local, heads, head_dim)
    )
    gate = jax.nn.sigmoid(proj[..., 3 * inner :])
    bias_part = jnp.einsum("kic,ch->hki", yn, w_bias, preferred_element_type=jnp.float32).astype(
        jnp.bfloat16
    )
    bias = lax.all_gather(bias_part, "dap", axis=2, tiled=True)
    scores = jnp.einsum(
        "irhd,krhd->rhki", query, keys, preferred_element_type=jnp.float32
    ) / jnp.sqrt(jnp.float32(head_dim))
    scores = scores + bias.astype(jnp.float32)[None]
    live = jnp.transpose(mask_cols.astype(jnp.float32))[:, None, :, None]
    scores = jnp.where(live > 0.5, scores, jnp.float32(-1000000000.0))
    weights = jax.nn.softmax(scores, axis=2).astype(jnp.bfloat16)
    summed = jnp.einsum(
        "rhki,krhd->irhd", weights, values, preferred_element_type=jnp.float32
    ).reshape(total, local, inner)
    att = (gate * summed).astype(jnp.bfloat16)
    return pair1 + matmul(att, w_att_out)


def split_shards(
    pair, pair_mask, w_left, w_right, w_tri_gate, w_tri_out, w_attend, w_bias, w_att_out
):
    hidden = w_tri_out.shape[0]
    maskf = pair_mask.astype(jnp.float32)
    zn = layer_norm(pair).astype(jnp.bfloat16)
    left_edge = edges(zn, w_left, maskf, hidden)
    right_edge = edges(zn, w_right, maskf, hidden)
    pair_cols, mask_cols = (
        lax.all_to_all(pair, "dap", split_axis=1, concat_axis=0, tiled=True),
        lax.all_to_all(
            pair_mask.astype(jnp.bfloat16), "dap", split_axis=1, concat_axis=0, tiled=True
        ),
    )
    tri = jnp.einsum(
        "ikc,jkc->ijc",
        lax.all_gather(left_edge, "dap", axis=0, tiled=True),
        right_edge,
        preferred_element_type=jnp.float32,
    )
    zn_cols = layer_norm(pair_cols).astype(jnp.bfloat16)
    pair1 = triangle_update(pair_cols, zn_cols, tri, w_tri_gate, w_tri_out)
    return attention(pair1, mask_cols, w_attend, w_bias, w_att_out)


def dot(a, b):
    return lax.dot_general(a, b, (((1,), (0,)), ((), ())), preferred_element_type=F32)


def dot_t(a, b):
    return lax.dot_general(a, b, (((1,), (1,)), ((), ())), preferred_element_type=F32)


def norm(x):
    width = x.shape[-1]
    mean = jnp.sum(x, axis=-1, keepdims=True) * (1.0 / width)
    x = x - mean
    var = jnp.sum(x * x, axis=-1, keepdims=True) * (1.0 / width)
    return x * lax.rsqrt(var + 1e-05)


def sigmoid(x):
    return 1.0 / (1.0 + jnp.exp(-x))


def iota(shape, dim):
    return lax.broadcasted_iota(jnp.int32, shape, dim)


def onehot(cond):
    return jnp.where(cond, 1.0, 0.0).astype(BF16)


def pad8(n):
    return -(-n // 8) * 8


def step(axis, rows, *refs, dims):
    count, total, local, heads = dims
    messages, weights, out_ref = refs[:count], refs[count : count + 7], refs[count + 7]
    w_left, w_right, w_tri_gate, w_tri_out, w_attend, w_bias, w_att_out = weights
    xs, ls, rs, ys, ps, ks, ms = refs[count + 8 :]
    width, hidden, inner = xs.shape[1], w_tri_out.shape[0], w_att_out.shape[0]
    head_dim = inner // heads
    pairs, held, every = rows * total, pad8(rows), total * total
    own = lax.axis_index(axis)

    for at, message in zip(order(own, count, rows, local), messages, strict=True):
        xs[pl.ds(pl.multiple_of(at * pairs, 8), pairs), :] = message[pl.ds(0, pairs), :].astype(F32)
        ms[pl.ds(pl.multiple_of(at * held, 8), held), :] = message[pl.ds(pairs, held), :].astype(F32)
    marks = ms[...].astype(BF16)
    shape = (every, marks.shape[0])
    residue = iota(shape, 0) // total
    spread = onehot(iota(shape, 1) == (residue // rows) * held + residue % rows)
    shape = (every, width)
    lanes = jnp.where(iota(shape, 1) == iota(shape, 0) % total, dot(spread, marks), 0.0)
    mask = dot(lanes.astype(BF16), jnp.ones((width, hidden), BF16))
    ks[...] = mask

    x = xs[...]
    zn = norm(x).astype(BF16)
    both = dot(zn, w_right[...])
    rs[...] = (sigmoid(both[:, :hidden]) * both[:, hidden:] * mask).astype(BF16).astype(F32)
    both = dot(zn, w_left[...])
    ls[...] = (sigmoid(both[:, :hidden]) * both[:, hidden:] * mask).astype(BF16).astype(F32)
    opened = sigmoid(dot(zn, w_tri_gate[...]))
    rights = [rs[pl.ds(k, total, stride=total), :] for k in range(total)]
    tri = []
    for i in range(total):
        terms = [ls[pl.ds(i * total + k, 1), :] * rights[k] for k in range(total)]
        tri.append(functools.reduce(lambda a, b: a + b, terms))
    tn = norm(jnp.concatenate(tri, axis=0)).astype(BF16)
    pair1 = x + opened * dot(tn, w_tri_out[...])
    ps[...] = pair1
    yf = norm(pair1)
    ys[...] = yf
    yn = yf.astype(BF16)

    mine = [pl.ds(own * local + j, total, stride=total) for j in range(local)]
    proj = dot(jnp.concatenate([ys[m, :] for m in mine], axis=0).astype(BF16), w_attend[...])
    query = proj[:, :inner].astype(BF16).astype(F32)
    key = proj[:, inner : 2 * inner].astype(BF16)
    value = proj[:, 2 * inner : 3 * inner].astype(BF16)
    gate = sigmoid(proj[:, 3 * inner :])
    lines, keys = local * heads * total, local * total
    head_of = iota((total, inner), 1) // head_dim
    queries = [
        jnp.where(head_of == h, query[j * total : (j + 1) * total], 0.0)
        for j in range(local)
        for h in range(heads)
    ]
    scores = dot_t(jnp.concatenate(queries, axis=0).astype(BF16), key) * (head_dim**-0.5)
    wb = w_bias[...].astype(F32)
    wb = [jnp.broadcast_to(wb[h : h + 1], (total, width)) for h in range(heads)]
    bias = dot_t(jnp.concatenate(wb, axis=0).astype(BF16), yn)
    shape = (heads * total, every)
    bias = jnp.where(iota(shape, 1) % total == iota(shape, 0) % total, bias, 0.0).astype(BF16)
    shape = (every, keys)
    bias = dot(bias, onehot(iota(shape, 0) // total == iota(shape, 1) % total))
    scores = scores + jnp.concatenate([bias] * local, axis=0)
    seen = jnp.concatenate([ks[m, :] for m in mine], axis=0)
    shape = (keys, hidden)
    seen = jnp.where(iota(shape, 1) == iota(shape, 0) // total, seen, 0.0).astype(BF16)
    shape = (lines, hidden)
    live = dot_t(onehot(iota(shape, 1) == iota(shape, 0) // (heads * total)), seen)
    scores = jnp.where(live > 0.5, scores, -1000000000.0)
    weights = jnp.exp(scores - jnp.max(scores, axis=-1, keepdims=True)).astype(BF16)
    sums = dot(weights, jnp.concatenate([value, jnp.ones_like(value)], axis=1))
    parts = []
    for j in range(local):
        part = None
        for h in range(heads):
            block = sums[(j * heads + h) * total : (j * heads + h + 1) * total]
            part = block if part is None else jnp.where(wide_head(total, inner, head_dim) == h, block, part)
        parts.append(part[:, :inner] / part[:, inner:])
    att = (gate * jnp.concatenate(parts, axis=0)).astype(BF16)
    out = dot(att, w_att_out[...])
    for j, m in enumerate(mine):
        out_ref[pl.ds(j, total, stride=local), :] = ps[m, :] + out[j * total : (j + 1) * total]


def wide_head(total, inner, head_dim):
    return (iota((total, 2 * inner), 1) % inner) // head_dim


def order(own, count, rows, local):
    if MODE == "hh":
        chip = own // (rows // local)
        return [chip ^ d for d in range(count)]
    return list(range(count))


def pack(pair_ref, mask_ref, out_ref, ms):
    pairs = pair_ref.shape[0]
    rows, total = mask_ref.shape
    ms[...] = jnp.zeros_like(ms)
    ms[pl.ds(0, rows), pl.ds(0, total)] = mask_ref[...].astype(F32)
    for c in range(out_ref.shape[0]):
        out_ref[c, pl.ds(0, pairs), :] = pair_ref[...]
        out_ref[c, pl.ds(pairs, ms.shape[0]), :] = ms[...].astype(BF16)


def pack2(axis, pair_ref, pair2_ref, mask_ref, mask2_ref, out_ref, ms):
    pairs = pair_ref.shape[0]
    rows, total = mask_ref.shape
    side = lax.rem(lax.axis_index(axis), 2)
    ms[...] = jnp.zeros_like(ms)
    for s, (p, m) in ((side, (pair_ref, mask_ref)), (1 - side, (pair2_ref, mask2_ref))):
        out_ref[pl.ds(pl.multiple_of(s * pairs, 8), pairs), :] = p[...]
        ms[pl.ds(s * rows, rows), pl.ds(0, total)] = m[...].astype(F32)
    out_ref[pl.ds(2 * pairs, ms.shape[0]), :] = ms[...].astype(BF16)


def call(kernel, shape, dtype, scratch, args):
    return pl.pallas_call(
        kernel,
        out_shape=jax.ShapeDtypeStruct(shape, dtype),
        in_specs=[VMEM] * len(args),
        out_specs=VMEM,
        scratch_shapes=scratch,
        compiler_params=pltpu.CompilerParams(vmem_limit_bytes=LIMIT),
    )(*args)


def whole_step(axis, n, pair, pair_mask, w_left, w_right, w_tri_gate, w_tri_out, w_attend, w_bias, w_att_out):
    local, total, width = pair.shape
    heads = w_bias.shape[1]
    hidden = w_tri_out.shape[0]
    flat = pair.reshape(local * total, width)
    rows = local
    if MODE in ("a2a", "ag"):
        copies = n if MODE == "a2a" else 1
        held = pad8(rows)
        msg = call(pack, (copies, rows * total + held, width), BF16, [pltpu.VMEM((held, width), F32)], (flat, pair_mask))
        if MODE == "a2a":
            got = lax.all_to_all(msg, axis, split_axis=0, concat_axis=0, tiled=True)
        else:
            got = lax.all_gather(msg, axis, axis=0, tiled=True)
        kernel = functools.partial(step_one, axis, rows, dims=(n, total, local, heads))
        messages = (got,)
        count = n
    else:
        swap = lambda x, d: lax.ppermute(x, axis, [(s, s ^ d) for s in range(n)])
        flat2, mask2 = swap(flat, 1), swap(pair_mask, 1)
        rows = 2 * local
        held = pad8(rows)
        msg = call(functools.partial(pack2, axis), (rows * total + held, width), BF16, [pltpu.VMEM((held, width), F32)], (flat, flat2, pair_mask, mask2))
        messages = (msg,) + tuple(swap(msg, 2 * d) for d in range(1, n // 2))
        count = n // 2
        kernel = functools.partial(step, axis, rows, dims=(count, total, local, heads))
    every = total * total
    scratch = [pltpu.VMEM((every, width), F32)] + [pltpu.VMEM((every, hidden), F32)] * 2 + [pltpu.VMEM((every, width), F32)] * 2 + [pltpu.VMEM((every, hidden), F32), pltpu.VMEM((count * held, width), F32)]
    out = call(kernel, (total * local, width), F32, scratch, messages + (w_left, w_right, w_tri_gate, w_tri_out, w_attend, w_bias.T, w_att_out))
    return out.reshape(total, local, width)


def step_one(axis, rows, got, *refs, dims):
    return step(axis, rows, *[got.at[c] for c in range(dims[0])], *refs, dims=dims)


def shards(axis, n, *args):
    local, total, width = args[0].shape
    hidden, inner, heads = args[5].shape[0], args[8].shape[0], args[7].shape[1]
    small = total * total <= 512 and total <= width == hidden == inner and width % 128 == 0 and total % 8 == 0 and n % 2 == 0 and n & (n - 1) == 0 and n <= 8
    return whole_step(axis, n, *args) if small else split_shards(*args)


def solution(mesh):
    placed = (P(("dp", "dap"), None, None), P(("dp", "dap"), None)) + (P(),) * 7
    return jax.shard_map(
        functools.partial(shards, "dap", mesh.shape["dap"]), mesh=mesh, in_specs=placed, out_specs=P("dp", "dap", None), check_vma=False
    )
```
